128 devices in a mesh: row: 8 (over y_lo, z), col: 16 (over x, y_hi, core).
Axes of the slice: x: 4, y: 4 (y_hi: 2, y_lo: 2; y = y_hi * 2 + y_lo), z: 4, core: 2. Of those that a mesh axis runs over, the one named last changes fastest.
Arguments:
- tiles: bfloat16 [8, 16, 96, 256, 256], P('row', 'col'), may hold values from 0 to 1
- tile_coord: int32 [8, 16, 96, 2], P('row', 'col'), may hold values from 0 to 15, as said below
- tile_count: int32 [8, 16], P('row', 'col'), may hold values from 0 to 96, as said below
- factors: bfloat16 [32768, 256], P(('row', 'col')), may hold values from -0.0625 to 0.0625
- owner: int32 [32768], P(('row', 'col')), may hold values from 0 to 32767, as said below
- gram_inverse: float32 [256, 256], replicated, as said below
Outputs:
- solution: float32 [32768, 256], P(('row', 'col'))
The draws below stay inside these ranges and needn't reach their ends.
Inputs may be any that keep to these rules, and one draw needn't show every extreme that they name: `tile_coord`: slots below a block's count hold distinct tile positions with r * 16 + i <= c * 8 + j; later slots are unused. Some block has all 96 slots used; blocks below the diagonal have none. `tile_count`: at most 96, reached in every draw. `owner`: A permutation of 0 to 32767; each block of 256 consecutive words has exactly 2 words whose value divided by 256 is d, for every device d. `gram_inverse`: Symmetric.
All inputs are finite; a program needn't handle non-finite values.
Results may differ from the reference program's by a relative error of at most 0.0003.
Values may be sent and summed in bfloat16 or wider, within the bound.
No kernel may reach another device: no remote copies, remote signals or barrier semaphores. Data moves between devices by JAX's collectives and lax.ppermute only.
A program may use at most 128 MiB of HBM per device.

```python
import math
import jax
import jax.numpy as jnp
from jax import lax

K = 256
TILE = 256
TR = 16
NNZ = 96
TC = 8
V = 32768
OWN = 256
SHARE = 2
N_ROW = 8
N_COL = 16
DEVICES = 128


def tile_layout(key):
    key_noise, key_want = jax.random.split(jax.random.fold_in(key, 7))
    row_ids = jnp.arange(N_ROW, dtype=jnp.int32)[:, None, None, None]
    col_ids = jnp.arange(N_COL, dtype=jnp.int32)[None, :, None, None]
    tile_i = jnp.arange(TR, dtype=jnp.int32)[None, None, :, None]
    tile_j = jnp.arange(TC, dtype=jnp.int32)[None, None, None, :]
    allowed = row_ids * TR + tile_i <= col_ids * TC + tile_j
    allowed = allowed.reshape(N_ROW, N_COL, TR * TC)
    noise = jax.random.randint(key_noise, (N_ROW, N_COL, TR * TC), 0, 1 << 16)
    scores = noise * (TR * TC) + jnp.arange(TR * TC, dtype=jnp.int32) + jnp.where(allowed, 0, (1 << 16) * (TR * TC))
    picked = jnp.argsort(scores, axis=-1)[..., :NNZ].astype(jnp.int32)
    coords = jnp.stack([picked // TC, picked % TC], axis=-1).astype(jnp.int32)
    possible = jnp.sum(allowed.astype(jnp.int32), axis=-1)
    row_top = NNZ - NNZ * jnp.arange(N_ROW, dtype=jnp.int32)[:, None] // N_ROW
    low_end = jnp.broadcast_to(row_top // 2, (N_ROW, N_COL))
    high_end = jnp.broadcast_to(row_top + 1, (N_ROW, N_COL))
    wanted = jax.random.randint(key_want, (N_ROW, N_COL), low_end, high_end).astype(jnp.int32)
    wanted = wanted.at[0, N_COL - 1].set(NNZ)
    counts = jnp.minimum(possible, wanted).astype(jnp.int32)
    return (coords, counts)


def draw_tile_coord(key, part):
    return tile_layout(key)[0]


def draw_tile_count(key, part):
    return tile_layout(key)[1]


def draw_owner(key, part):
    key_piece, key_slot = jax.random.split(jax.random.fold_in(key, 11))
    piece_scores = jax.random.randint(key_piece, (DEVICES, OWN), 0, 1 << 20) * OWN + jnp.arange(OWN, dtype=jnp.int32)
    placing = jnp.argsort(piece_scores, axis=-1).astype(jnp.int32)
    dest_ids = placing // SHARE
    within = placing % SHARE
    piece_ids = jnp.arange(DEVICES, dtype=jnp.int32)[:, None]
    first_slot = piece_ids * SHARE + within
    slot_scores = jax.random.randint(key_slot, (DEVICES, OWN), 0, 1 << 20) * OWN + jnp.arange(OWN, dtype=jnp.int32)
    slot_perm = jnp.argsort(slot_scores, axis=-1).astype(jnp.int32)
    final_slot = slot_perm[dest_ids, first_slot]
    return (dest_ids * OWN + final_slot).reshape(V).astype(jnp.int32)


def draw_gram_inverse(key, part):
    key_diag, key_off = jax.random.split(jax.random.fold_in(key, 5))
    diag_vals = jnp.exp(jax.random.uniform(key_diag, (K,), jnp.float32, math.log(0.5), math.log(2.0)))
    noise = jax.random.normal(key_off, (K, K), jnp.float32)
    off_part = (noise + noise.T) * (0.25 / math.sqrt(K))
    return jnp.diag(diag_vals) + off_part


def level_of(stream_key, shape, shards, smallest, largest):
    gain, own = 1.0, jax.random.fold_in(stream_key, 6)
    for position, parts in shards:
        heights = jnp.exp(jax.random.uniform(jax.random.fold_in(own, position), (parts,), jnp.float32, smallest / len(shards), largest / len(shards)))
        gain = gain * jnp.repeat(heights, shape[position] // parts).reshape([-1 if axis == position else 1 for axis in range(len(shape))])
    return gain


def normal_values(own_key, dims, width, most, cuts=(), held_as=jnp.bfloat16):
    drawn = width * jax.random.normal(own_key, dims, jnp.float32)
    if cuts:
        drawn = drawn * level_of(own_key, dims, cuts, -0.22, 0.18)
    return jnp.clip(drawn, -most, most).astype(held_as)


def setup_inputs(seed: int = 0) -> dict:
    key_list = jax.random.split(jax.random.key(seed), 7)
    tiles = jnp.clip(1.0 * jax.random.uniform(key_list[0], (N_ROW, N_COL, NNZ, TILE, TILE), jnp.float32) ** level_of(key_list[0], (N_ROW, N_COL, NNZ, TILE, TILE), ((0, 8), (1, 16)), -0.2, 0.2), 0.0, 1.0).astype(jnp.bfloat16)
    tile_coord = draw_tile_coord(jax.random.fold_in(key_list[6], 71), 0)
    tile_count = draw_tile_count(jax.random.fold_in(key_list[6], 71), 0)
    factors = normal_values(key_list[3], (V, K), (V // 4) ** -0.5, 0.0625, ((0, 128),))
    owner = draw_owner(jax.random.fold_in(key_list[6], 71), 0)
    gram_inverse = draw_gram_inverse(jax.random.fold_in(key_list[6], 71), 0)
    return dict(tiles=tiles, tile_coord=tile_coord, tile_count=tile_count, factors=factors, owner=owner, gram_inverse=gram_inverse)


def add_rows(accum, start_row, term):
    width_rows = term.shape[0]
    current = lax.dynamic_slice_in_dim(accum, start_row, width_rows, 0)
    return lax.dynamic_update_slice_in_dim(accum, current + term, start_row, 0)


def reference(tiles, tile_coord, tile_count, factors, owner, gram_inverse):
    tile_dim = tiles.shape[-1]
    rank_dim = factors.shape[1]
    flat_tiles = tiles.reshape(N_ROW * N_COL, NNZ, tile_dim, tile_dim)
    flat_coords = tile_coord.reshape(N_ROW * N_COL, NNZ, 2)
    flat_counts = tile_count.reshape(N_ROW * N_COL)

    def device_step(product, device):
        row_block = device // N_COL
        col_block = device % N_COL
        dev_tiles = lax.dynamic_index_in_dim(flat_tiles, device, 0, False)
        dev_coords = lax.dynamic_index_in_dim(flat_coords, device, 0, False)

        def tile_step(slot_idx, accum):
            x_tile = lax.dynamic_index_in_dim(dev_tiles, slot_idx, 0, False)
            where_now = lax.dynamic_index_in_dim(dev_coords, slot_idx, 0, False)
            tile_p = (row_block * TR + where_now[0]).astype(jnp.int32)
            tile_q = (col_block * TC + where_now[1]).astype(jnp.int32)
            start_p = (tile_p * tile_dim).astype(jnp.int32)
            start_q = (tile_q * tile_dim).astype(jnp.int32)
            w_q = lax.dynamic_slice_in_dim(factors, start_q, tile_dim, 0)
            w_p = lax.dynamic_slice_in_dim(factors, start_p, tile_dim, 0)
            accum = add_rows(accum, start_p, jnp.dot(x_tile, w_q, preferred_element_type=jnp.float32))
            upper_mask = (tile_p < tile_q).astype(jnp.float32)
            mirrored = jnp.dot(x_tile.T, w_p, preferred_element_type=jnp.float32)
            return add_rows(accum, start_q, upper_mask * mirrored)

        return lax.fori_loop(0, flat_counts[device], tile_step, product), None

    start_sum = jnp.zeros((V, rank_dim), jnp.float32)
    product, _ = lax.scan(device_step, start_sum, jnp.arange(N_ROW * N_COL, dtype=jnp.int32))
    solved = jnp.dot(product, gram_inverse, precision=lax.Precision.HIGHEST)
    return jnp.zeros((V, rank_dim), jnp.float32).at[owner].set(solved)
```

```python
import jax
import jax.numpy as jnp
from jax import lax
from jax.experimental import pallas as pl
from jax.experimental.pallas import tpu as pltpu
from jax.sharding import PartitionSpec as P


K = 256
T = 256
TR = 16
TC = 8
NNZ = 96
AUX = 16
BLK = T + AUX
DEV = 128
ROWS = 80
HI = lax.Precision.HIGHEST


def tile_kernel(n_par, where, meta, tiles, *refs):
    panels = refs[:12]
    send_ref, keep_ref, yt_ref, aux_ref = refs[12:16]
    dense, rmat, rt, cmat, raux, caux, used, tsem, bsem = refs[16:]
    count, row_at, col_at = meta[0], meta[1], meta[2]
    core = lax.rem(col_at, 2)
    chip = col_at // 2
    x_at, y_at = chip // 2, lax.rem(chip, 2)
    lo_at, z_at = row_at // 4, lax.rem(row_at, 4)

    copies = []
    for group in range(3):
        for s in range(4):
            for second in range(2):
                src = panels[4 * group + s].at[second]
                if group < 2:
                    xx = lax.rem(x_at + 4 - s, 4)
                    yy = 1 - y_at if second else y_at
                    hh = core if group == 0 else 1 - core
                    at = xx * 4 + yy * 2 + hh
                    data, extra = rmat.at[at], raux.at[at]
                else:
                    zz = lax.rem(z_at + 4 - s, 4)
                    ll = 1 - lo_at if second else lo_at
                    at = ll * 4 + zz
                    data, extra = cmat.at[pl.ds(at * T, T)], caux.at[at]
                n = 2 * len(copies)
                copies.append(
                    (
                        pltpu.make_async_copy(src.at[pl.ds(0, T)], data, bsem.at[n]),
                        pltpu.make_async_copy(src.at[pl.ds(T, AUX)], extra, bsem.at[n + 1]),
                    )
                )
    for pair in copies:
        pair[0].start()
        pair[1].start()

    def clear(n, _):
        used[n] = 0
        return 0

    lax.fori_loop(0, TR * TC, clear, 0)

    def tile_copy(s):
        i, j = where[2 * s], where[2 * s + 1]
        return i, j, pltpu.make_async_copy(
            tiles.at[s],
            dense.at[pl.ds(pl.multiple_of(i * T, T), T), pl.ds(pl.multiple_of(j * T, T), T)],
            tsem.at[s],
        )

    def start(s, _):
        i, j, copy = tile_copy(s)
        copy.start()
        used[i * TC + j] = 1
        return 0

    lax.fori_loop(0, count, start, 0)

    def blank(n, _):
        @pl.when(used[n] == 0)
        def _():
            i, j = n // TC, lax.rem(n, TC)
            dense[
                pl.ds(pl.multiple_of(i * T, T), T), pl.ds(pl.multiple_of(j * T, T), T)
            ] = jnp.zeros((T, T), jnp.bfloat16)

        return 0

    lax.fori_loop(0, TR * TC, blank, 0)
    for pair in copies:
        pair[0].wait()
        pair[1].wait()

    for i in range(TR):
        rt[:, i * T : (i + 1) * T] = rmat[i].T
    for b in range(TC):
        aux_ref[b : b + 1, :] = raux[core * TC + b, 0:1, :].astype(jnp.float32)
        aux_ref[TC + b : TC + b + 1, :] = caux[b, 0:1, :].astype(jnp.float32)
        aux_ref[2 * TC + b : 2 * TC + b + 1, :] = raux[core * TC + b, 1:2, :].astype(jnp.float32)

    def wait(s, _):
        tile_copy(s)[2].wait()
        return 0

    lax.fori_loop(0, count, wait, 0)

    for out_ref, base in ((send_ref, 1 - core), (keep_ref, core)):
        def rows(q, _, out_ref=out_ref, base=base):
            at = pl.multiple_of((base * TC + 2 * q) * T, T)
            out_ref[pl.ds(pl.multiple_of(q * 2 * T, T), 2 * T), :] = jnp.dot(
                dense[pl.ds(at, 2 * T), :], cmat[...], preferred_element_type=jnp.float32
            )
            return 0

        lax.fori_loop(0, TC // 2, rows, 0)

    @pl.when(row_at == chip)
    def _():
        for j in range(TC):
            at = pl.multiple_of((core * TC + j) * T, T)
            dense[pl.ds(at, T), j * T : (j + 1) * T] = jnp.zeros((T, T), jnp.bfloat16)

    def cols(j, _):
        yt_ref[pl.ds(pl.multiple_of(j * K, K), K), :] = jnp.dot(
            rt[...],
            dense[:, pl.ds(pl.multiple_of(j * T, T), T)],
            preferred_element_type=jnp.float32,
        )
        return 0

    lax.fori_loop(0, TC, cols, 0)


def tile_sums(tiles, where, meta, panels):
    any_spec = pl.BlockSpec(memory_space=pl.ANY)
    vmem = pl.BlockSpec(memory_space=pltpu.VMEM)
    smem = pl.BlockSpec(memory_space=pltpu.SMEM)
    f32 = jnp.float32
    return pl.pallas_call(
        lambda *refs: tile_kernel(0, *refs),
        out_shape=(
            jax.ShapeDtypeStruct((TC * T, K), f32),
            jax.ShapeDtypeStruct((TC * T, K), f32),
            jax.ShapeDtypeStruct((TC * K, T), f32),
            jax.ShapeDtypeStruct((3 * TC, T), f32),
        ),
        in_specs=[smem, smem, any_spec] + [any_spec] * 12,
        out_specs=(vmem, vmem, vmem, vmem),
        scratch_shapes=[
            pltpu.VMEM((TR * T, TC * T), jnp.bfloat16),
            pltpu.VMEM((TR, T, K), jnp.bfloat16),
            pltpu.VMEM((K, TR * T), jnp.bfloat16),
            pltpu.VMEM((TC * T, K), jnp.bfloat16),
            pltpu.VMEM((TR, AUX, T), jnp.bfloat16),
            pltpu.VMEM((TC, AUX, T), jnp.bfloat16),
            pltpu.SMEM((TR * TC,), jnp.int32),
            pltpu.SemaphoreType.DMA((NNZ,)),
            pltpu.SemaphoreType.DMA((48,)),
        ],
        cost_estimate=pl.CostEstimate(
            flops=8_600_000_000, bytes_accessed=22_000_000, transcendentals=0
        ),
        compiler_params=pltpu.CompilerParams(vmem_limit_bytes=48 << 20),
        name="tile_sums",
    )(where, meta, tiles, *panels)


def split_dot(pick, value, dims):
    high = value.astype(jnp.bfloat16)
    low = (value - high.astype(jnp.float32)).astype(jnp.bfloat16)
    first = lax.dot_general(pick, high, dims, preferred_element_type=jnp.float32)
    return first + lax.dot_general(pick, low, dims, preferred_element_type=jnp.float32)


def code_kernel(meta, keep, got, yt, aux, out_ref, rows):
    row_at, core = meta[1], lax.rem(meta[2], 2)
    group = 2 * row_at + core
    pos_ids = lax.broadcasted_iota(jnp.int32, (T, T), 0).astype(jnp.float32)
    lane_ids = lax.broadcasted_iota(jnp.int32, (128, T), 0)
    nn, nt = (((1,), (0,)), ((), ())), (((1,), (1,)), ((), ()))
    peaks = [jnp.zeros((8, 128), jnp.float32)] * 2
    slots = jnp.zeros((DEV, 128), jnp.float32)
    offset = lax.rem(group, 8) * 16
    for part in range(2):
        for b in range(TC):
            line = part * TC + b
            pick = (pos_ids == aux[line : line + 1, :]).astype(jnp.bfloat16)
            at = slice(b * T, (b + 1) * T)
            if part == 0:
                value = split_dot(pick, keep[at, :] + got[at, :], nn)
            else:
                value = split_dot(pick, yt[at, :], nt)
            peaks[part] = jnp.maximum(
                peaks[part], jnp.max(jnp.abs(value.reshape(-1, 8, 2, 128)), axis=(0, 2))
            )
            for t in range(2):
                half = slice(t * DEV, (t + 1) * DEV)
                for side in range(2):
                    rows[pl.ds(32 * part + 16 * side + 2 * b + t, DEV, stride=ROWS), :] = value[
                        half, side * 128 : (side + 1) * 128
                    ]
                if part == 0:
                    lanes = jnp.where(
                        lane_ids == offset + (2 * b + t), aux[2 * TC + b : 2 * TC + b + 1, :], 0.0
                    ).astype(jnp.bfloat16)
                    slots += lax.dot_general(
                        pick[half, :], lanes, nt, preferred_element_type=jnp.float32
                    )
    low_half = group < 8
    rows[pl.ds(64, DEV, stride=ROWS), :] = jnp.where(low_half, slots, 0.0)
    rows[pl.ds(65, DEV, stride=ROWS), :] = jnp.where(low_half, 0.0, slots)
    scales = []
    for part in range(2):
        peak = jnp.max(peaks[part], axis=(0, 1), keepdims=True)
        peak = jnp.broadcast_to(jnp.maximum(peak, 1e-30), (8, 128))
        power = jnp.clip(jnp.floor(jnp.log2(32000.0 / peak)), -100.0, 100.0)
        scales.append(jnp.exp2(power)[0:1, :])
        rows[pl.ds(66 + part, DEV, stride=ROWS), :] = jnp.broadcast_to(power[0:1, :], (DEV, 128))
    for line in range(68, ROWS):
        rows[pl.ds(line, DEV, stride=ROWS), :] = jnp.zeros((DEV, 128), jnp.float32)

    def code(value):
        return jnp.floor(value + 0.5).astype(jnp.int32).astype(jnp.int16)

    def to_one(d, _):
        at = d * ROWS
        out_ref[d, 0:32, :] = code(rows[pl.ds(pl.multiple_of(at, 8), 32), :] * scales[0])
        out_ref[d, 32:64, :] = code(rows[pl.ds(pl.multiple_of(at + 32, 8), 32), :] * scales[1])
        out_ref[d, 64:80, :] = code(rows[pl.ds(pl.multiple_of(at + 64, 8), 16), :])
        return 0

    lax.fori_loop(0, DEV, to_one, 0, unroll=4)


def code_rows(meta, keep, got, yt, aux):
    vmem = pl.BlockSpec(memory_space=pltpu.VMEM)
    return pl.pallas_call(
        code_kernel,
        out_shape=jax.ShapeDtypeStruct((DEV, ROWS, 128), jnp.int16),
        in_specs=[pl.BlockSpec(memory_space=pltpu.SMEM)] + [vmem] * 4,
        out_specs=vmem,
        scratch_shapes=[pltpu.VMEM((DEV * ROWS, 128), jnp.float32)],
        compiler_params=pltpu.CompilerParams(vmem_limit_bytes=40 << 20),
        name="code_rows",
    )(meta, keep, got, yt, aux)


def solve_kernel(got, gram, out_ref, sums, slots):
    sums[...] = jnp.zeros_like(sums)
    slots[...] = jnp.zeros_like(slots)

    def source_row(r, _):
        for c in range(16):
            value = got[r * 16 + c].astype(jnp.int32).astype(jnp.float32)
            scale_x = jnp.exp2(-value[66:67, :])
            scale_y = jnp.exp2(-value[67:68, :])
            sums[2 * r + c % 2] += value[0:32, :] * scale_x
            sums[c] += value[32:64, :] * scale_y
            if c < 2:
                slots[...] += value[64:72, :]
        return 0

    lax.fori_loop(0, 8, source_row, 0)
    product = jnp.concatenate(
        [sums[:, 0:16, :].reshape(256, 128), sums[:, 16:32, :].reshape(256, 128)], axis=1
    )
    where = jnp.concatenate([slots[0:1, :], slots[1:2, :]], axis=1)
    ids = lax.broadcasted_iota(jnp.int32, (256, 256), 0).astype(jnp.float32)
    pick = (ids == where).astype(jnp.float32)
    placed = jnp.dot(pick, product, precision=HI, preferred_element_type=jnp.float32)
    out_ref[...] = jnp.dot(placed, gram[...], precision=HI, preferred_element_type=jnp.float32)


def solve_rows(got, gram):
    vmem = pl.BlockSpec(memory_space=pltpu.VMEM)
    return pl.pallas_call(
        solve_kernel,
        out_shape=jax.ShapeDtypeStruct((256, 256), jnp.float32),
        in_specs=[vmem, vmem],
        out_specs=vmem,
        scratch_shapes=[
            pltpu.VMEM((16, 32, 128), jnp.float32),
            pltpu.VMEM((8, 128), jnp.float32),
        ],
        compiler_params=pltpu.CompilerParams(vmem_limit_bytes=32 << 20),
        name="solve_rows",
    )(got, gram)


def along_x(shift):
    return [(c, (c + 4 * shift) % 16) for c in range(16)]


def along_z(shift):
    return [(r, (r // 4) * 4 + (r + shift) % 4) for r in range(8)]


def to_columns(flip):
    pairs = []
    for r in range(8):
        for c in range(16):
            h, j = c // 8, c % 8
            pairs.append((16 * r + c, 16 * (j ^ flip) + 2 * r + h))
    return pairs


def per_device(tiles, tile_coord, tile_count, factors, owner, gram_inverse):
    row_at = lax.axis_index("row")
    col_at = lax.axis_index("col")
    dest = owner // T
    words = jnp.arange(T, dtype=jnp.int32)
    earlier = (dest[:, None] == dest[None, :]) & (words[None, :] < words[:, None])
    second = jnp.any(earlier, axis=1).astype(jnp.int32)
    place = (second * DEV + dest).astype(jnp.bfloat16)
    slot = (owner % T).astype(jnp.bfloat16)
    extra = jnp.concatenate(
        [place[None], slot[None], jnp.zeros((AUX - 2, T), jnp.bfloat16)], axis=0
    )
    block = jnp.concatenate([factors, extra], axis=0)

    both = ("row", "col")
    core_swap = [(c, c ^ 1) for c in range(16)]
    col_pair = jnp.stack(
        [lax.ppermute(block, both, to_columns(0)), lax.ppermute(block, both, to_columns(4))]
    )
    row_pair = jnp.stack([block, lax.ppermute(block, "col", [(c, c ^ 2) for c in range(16)])])
    mine = [row_pair] + [lax.ppermute(row_pair, "col", along_x(s)) for s in (1, 2, 3)]
    down = [col_pair] + [lax.ppermute(col_pair, "row", along_z(s)) for s in (1, 2, 3)]
    other = [lax.ppermute(panel, "col", core_swap) for panel in mine]

    meta = jnp.stack([tile_count[0, 0], row_at, col_at]).astype(jnp.int32)
    send, keep, yt, aux = tile_sums(
        tiles[0, 0], tile_coord[0, 0].reshape(-1), meta, mine + other + down
    )
    got = lax.ppermute(send, "col", core_swap)
    coded = code_rows(meta, keep, got, yt, aux)
    moved = lax.all_to_all(coded, both, 0, 0, tiled=True)
    return solve_rows(moved, gram_inverse)


def solution(mesh):
    in_specs = (
        P("row", "col", None, None, None),
        P("row", "col", None, None),
        P("row", "col"),
        P(("row", "col"), None),
        P(("row", "col")),
        P(),
    )
    return jax.shard_map(
        per_device,
        mesh=mesh,
        in_specs=in_specs,
        out_specs=P(("row", "col"), None),
        check_vma=False,
    )
```

```python
import jax
import jax.numpy as jnp
from jax import lax
from jax.experimental import pallas as pl
from jax.experimental.pallas import tpu as pltpu
from jax.sharding import PartitionSpec as P


K = 256
T = 256
TR = 16
TC = 8
NNZ = 96
CHUNK = 8
AUX = 16
BLK = T + AUX
DEV = 128
ROWS = 72
HI = lax.Precision.HIGHEST
VMEM = pl.BlockSpec(memory_space=pltpu.VMEM)
SMEM = pl.BlockSpec(memory_space=pltpu.SMEM)
F32 = jnp.float32
BF16 = jnp.bfloat16


def position(meta):
    row_at, col_at = meta[1], meta[2]
    chip = col_at // 2
    return (
        lax.rem(col_at, 2),
        chip // 2,
        lax.rem(chip, 2),
        row_at // 4,
        lax.rem(row_at, 4),
    )


def row_panel_at(meta, n):
    core, x_at, y_at, _, _ = position(meta)
    xx = lax.rem(x_at + 4 - (n // 2) % 4, 4)
    yy = 1 - y_at if n % 2 else y_at
    hh = 1 - core if n // 8 else core
    return xx * 4 + yy * 2 + hh


def col_panel_at(meta, n):
    _, _, _, lo_at, z_at = position(meta)
    zz = lax.rem(z_at + 4 - n // 2, 4)
    return (1 - lo_at if n % 2 else lo_at) * 4 + zz


def chunk_copy(tiles, held, sems, c):
    at = pl.ds(c * CHUNK, CHUNK)
    return pltpu.make_async_copy(tiles.at[at], held.at[at], sems.at[c])


def over_tiles(count, tiles, held, sems, fill, step):
    for c in range(NNZ // CHUNK):
        chunk_copy(tiles, held, sems, c).start()
    fill()

    def chunk(c, _):
        chunk_copy(tiles, held, sems, c).wait()
        for u in range(CHUNK):
            step(c * CHUNK + u)
        return 0

    chunks = (count + CHUNK - 1) // CHUNK
    lax.fori_loop(0, chunks, chunk, 0)

    def rest(c, _):
        chunk_copy(tiles, held, sems, c).wait()
        return 0

    lax.fori_loop(chunks, NNZ // CHUNK, rest, 0)


def tile_kernel(where, meta, tiles, *refs):
    row_panels, col_panels, refs = refs[:8], refs[8:16], refs[16:]
    yt_ref, away_ref, own_ref, row_aux, col_aux, rt, cmat, total, held, sems = refs
    count, first, left = meta[0], meta[1] * TR, meta[2] * TC
    shift = TC * (1 - position(meta)[0])

    def fill():
        yt_ref[...] = jnp.zeros_like(yt_ref)
        total[...] = jnp.zeros_like(total)
        rt[TR] = jnp.zeros((K, T), BF16)
        cmat[TC] = jnp.zeros((T, K), BF16)
        for n in range(8):
            at = col_panel_at(meta, n)
            cmat[at] = col_panels[n][0:T, :]
            col_aux[at] = col_panels[n][T:BLK, :]
        for n in range(16):
            at = row_panel_at(meta, n)
            rt[at] = row_panels[n // 2][n % 2, 0:T, :].T
            row_aux[at] = row_panels[n // 2][n % 2, T:BLK, :]

    def step(s):
        i, j = where[2 * s], where[2 * s + 1]
        use = s < count
        upper = jnp.logical_and(use, first + i < left + j)
        at = lax.rem(jnp.where(use, i, 0) + shift, TR)
        total[at] += jnp.dot(
            held[s], cmat[jnp.where(use, j, TC)], preferred_element_type=F32
        )
        at = pl.multiple_of(jnp.where(upper, j, 0) * K, K)
        yt_ref[pl.ds(at, K), :] += jnp.dot(
            rt[jnp.where(upper, i, TR)], held[s], preferred_element_type=F32
        )

    over_tiles(count, tiles, held, sems, fill, step)
    for b in range(TC):
        away_ref[b * T : (b + 1) * T, :] = total[b]
        own_ref[b * T : (b + 1) * T, :] = total[TC + b]


def tile_sums(where, meta, tiles, row_panels, col_panels):
    shapes = [jax.ShapeDtypeStruct((TC * T, K), F32)] * 3
    shapes += [jax.ShapeDtypeStruct((n, AUX, T), BF16) for n in (TR, TC)]
    return pl.pallas_call(
        tile_kernel,
        out_shape=shapes,
        in_specs=[SMEM, SMEM, pl.BlockSpec(memory_space=pltpu.HBM)] + [VMEM] * 16,
        out_specs=[VMEM] * 5,
        scratch_shapes=[
            pltpu.VMEM((TR + 1, K, T), BF16),
            pltpu.VMEM((TC + 1, T, K), BF16),
            pltpu.VMEM((TR, T, K), F32),
            pltpu.VMEM((NNZ, T, T), BF16),
            pltpu.SemaphoreType.DMA((NNZ // CHUNK,)),
        ],
        cost_estimate=pl.CostEstimate(
            flops=6_500_000_000, bytes_accessed=20_000_000, transcendentals=0
        ),
        compiler_params=pltpu.CompilerParams(vmem_limit_bytes=53 << 20),
        name="tile_sums",
    )(where, meta, tiles, *row_panels, *col_panels)


def split_dot(pick, value, dims):
    high = value.astype(BF16)
    low = (value - high.astype(F32)).astype(BF16)
    first = lax.dot_general(pick, high, dims, preferred_element_type=F32)
    return first + lax.dot_general(pick, low, dims, preferred_element_type=F32)


NN, NT = (((1,), (0,)), ((), ())), (((1,), (1,)), ((), ()))


def code(value):
    return jnp.floor(value + 0.5).astype(jnp.int32).astype(jnp.int16)


def sort_panel(is_x, meta, aux, rows, stride, block):
    core = position(meta)[0]
    base = TC * core if is_x else 0
    offset = lax.rem(2 * meta[1] + core, 8) * 16
    owners = lax.broadcasted_iota(jnp.int32, (DEV, T), 0).astype(F32)
    lane_ids = lax.broadcasted_iota(jnp.int32, (128, T), 0)
    before = (
        lax.broadcasted_iota(jnp.int32, (T, T), 0) < lax.broadcasted_iota(jnp.int32, (T, T), 1)
    ).astype(BF16)
    peak = jnp.zeros((8, 128), F32)
    slots = jnp.zeros((DEV, 128), F32)
    for b in range(TC):
        extra = aux[base + b].astype(F32)
        same = extra[0:1, :] == owners
        ranks = jnp.dot(same.astype(BF16), before, preferred_element_type=F32)
        value = block(b)
        for t in range(2):
            pick = (same & ((ranks > 0.5) if t else (ranks < 0.5))).astype(BF16)
            moved = split_dot(pick, value, NN if is_x else NT)
            for side in range(2):
                half = moved[:, side * 128 : (side + 1) * 128]
                peak = jnp.maximum(peak, jnp.max(jnp.abs(half.reshape(16, 8, 128)), axis=0))
                rows[pl.ds(16 * side + 2 * b + t, DEV, stride=stride), :] = half
            if is_x:
                lanes = jnp.where(lane_ids == offset + (2 * b + t), extra[1:2, :], 0.0)
                slots += lax.dot_general(
                    pick, lanes.astype(BF16), NT, preferred_element_type=F32
                )
    top = jnp.broadcast_to(
        jnp.maximum(jnp.max(peak, axis=(0, 1), keepdims=True), 1e-30), (8, 128)
    )
    power = jnp.clip(jnp.floor(jnp.log2(32000.0 / top)), -100.0, 100.0)
    return power, jnp.exp2(power)[0:1, :], slots


def code_y_kernel(meta, aux, yt, out_ref, power_ref, rows):
    power, scale, _ = sort_panel(
        False, meta, aux, rows, 32, lambda b: yt[b * T : (b + 1) * T, :]
    )
    power_ref[...] = power

    def to_one(d, _):
        out_ref[d] = code(rows[pl.ds(pl.multiple_of(d * 32, 32), 32), :] * scale)
        return 0

    lax.fori_loop(0, DEV, to_one, 0, unroll=8)


def code_y(meta, aux, yt):
    return pl.pallas_call(
        code_y_kernel,
        out_shape=(
            jax.ShapeDtypeStruct((DEV, 32, 128), jnp.int16),
            jax.ShapeDtypeStruct((8, 128), F32),
        ),
        in_specs=[SMEM] + [VMEM] * 2,
        out_specs=(VMEM, VMEM),
        scratch_shapes=[pltpu.VMEM((DEV * 32, 128), F32)],
        cost_estimate=pl.CostEstimate(
            flops=1_000_000_000, bytes_accessed=8_000_000, transcendentals=0
        ),
        compiler_params=pltpu.CompilerParams(vmem_limit_bytes=8 << 20),
        name="code_y",
    )(meta, aux, yt)


def code_x_kernel(meta, aux, own, got, coded_y, power_y, out_ref, rows):
    def block(b):
        at = slice(b * T, (b + 1) * T)
        return own[at, :] + got[at, :]

    power, scale, slots = sort_panel(True, meta, aux, rows, 40, block)
    low_half = 2 * meta[1] + position(meta)[0] < 8
    rows[pl.ds(32, DEV, stride=40), :] = jnp.where(low_half, slots, 0.0)
    rows[pl.ds(33, DEV, stride=40), :] = jnp.where(low_half, 0.0, slots)
    rows[pl.ds(34, DEV, stride=40), :] = jnp.broadcast_to(power[0:1, :], (DEV, 128))
    rows[pl.ds(35, DEV, stride=40), :] = jnp.broadcast_to(power_y[0:1, :], (DEV, 128))
    for line in range(36, 40):
        rows[pl.ds(line, DEV, stride=40), :] = jnp.zeros((DEV, 128), F32)

    def to_one(d, _):
        at = pl.multiple_of(d * 40, 8)
        out_ref[d, 0:32, :] = code(rows[pl.ds(at, 32), :] * scale)
        out_ref[d, 32:64, :] = coded_y[d]
        out_ref[d, 64:ROWS, :] = code(rows[pl.ds(at + 32, 8), :])
        return 0

    lax.fori_loop(0, DEV, to_one, 0, unroll=8)


def code_x(meta, aux, own, got, coded_y, power_y):
    return pl.pallas_call(
        code_x_kernel,
        out_shape=jax.ShapeDtypeStruct((DEV, ROWS, 128), jnp.int16),
        in_specs=[SMEM] + [VMEM] * 5,
        out_specs=VMEM,
        scratch_shapes=[pltpu.VMEM((DEV * 40, 128), F32)],
        cost_estimate=pl.CostEstimate(
            flops=1_000_000_000, bytes_accessed=8_000_000, transcendentals=0
        ),
        compiler_params=pltpu.CompilerParams(vmem_limit_bytes=8 << 20),
        name="code_x",
    )(meta, aux, own, got, coded_y, power_y)


def solve_kernel(got, gram, out_ref, sums, slots):
    sums[...] = jnp.zeros_like(sums)
    slots[...] = jnp.zeros_like(slots)

    def source_row(r, _):
        totals = [sums[2 * r], sums[2 * r + 1]]
        for c in range(16):
            value = got[r * 16 + c].astype(jnp.int32).astype(F32)
            totals[c % 2] += value[0:32, :] * jnp.exp2(-value[66:67, :])
            if c < 2:
                slots[...] += value[64:72, :]
        sums[2 * r] = totals[0]
        sums[2 * r + 1] = totals[1]
        for c in range(16):
            value = got[r * 16 + c].astype(jnp.int32).astype(F32)
            sums[c] += value[32:64, :] * jnp.exp2(-value[67:68, :])
        return 0

    lax.fori_loop(0, 8, source_row, 0)
    product = jnp.concatenate(
        [sums[:, 0:16, :].reshape(256, 128), sums[:, 16:32, :].reshape(256, 128)], axis=1
    )
    where = jnp.concatenate([slots[0:1, :], slots[1:2, :]], axis=1)
    ids = lax.broadcasted_iota(jnp.int32, (256, 256), 0).astype(F32)
    pick = (ids == where).astype(F32)
    placed = jnp.dot(pick, product, precision=HI, preferred_element_type=F32)
    out_ref[...] = jnp.dot(placed, gram[...], precision=HI, preferred_element_type=F32)


def solve_rows(got, gram):
    return pl.pallas_call(
        solve_kernel,
        out_shape=jax.ShapeDtypeStruct((256, 256), F32),
        in_specs=[VMEM] * 2,
        out_specs=VMEM,
        scratch_shapes=[pltpu.VMEM((16, 32, 128), F32), pltpu.VMEM((8, 128), F32)],
        compiler_params=pltpu.CompilerParams(vmem_limit_bytes=8 << 20),
        name="solve_rows",
    )(got, gram)


def along_x(shift):
    return [(c, (c + 4 * shift) % 16) for c in range(16)]


def along_z(shift):
    return [(r, (r // 4) * 4 + (r + shift) % 4) for r in range(8)]


CORE = [(c, c ^ 1) for c in range(16)]
UPPER_Y = [(c, c ^ 2) for c in range(16)]
LOWER_Y = [(r, r ^ 4) for r in range(8)]
TO_COLUMN = [
    (16 * r + c, 16 * (c % 8) + 2 * r + c // 8) for r in range(8) for c in range(16)
]


def per_device(tiles, tile_coord, tile_count, factors, owner, gram_inverse):
    both = ("row", "col")
    extra = jnp.stack([owner // T, owner % T]).astype(BF16)
    extra = jnp.concatenate([extra, jnp.zeros((AUX - 2, T), BF16)], axis=0)
    block = jnp.concatenate([factors, extra], axis=0)

    row_pair = jnp.stack([block, lax.ppermute(block, "col", UPPER_Y)])
    own = [row_pair] + [lax.ppermute(row_pair, "col", along_x(s)) for s in (1, 2, 3)]
    row_panels = own + [lax.ppermute(own[n], "col", CORE) for n in range(4)]
    first = lax.ppermute(block, both, TO_COLUMN)
    lower = lax.ppermute(first, "row", LOWER_Y)
    col_panels = [first, lower]
    for s in (1, 2, 3):
        col_panels += [
            lax.ppermute(first, "row", along_z(s)), lax.ppermute(lower, "row", along_z(s))
        ]

    row_at, col_at = lax.axis_index("row"), lax.axis_index("col")
    meta = jnp.stack([tile_count[0, 0], row_at, col_at]).astype(jnp.int32)
    where = tile_coord[0, 0].reshape(-1)
    slabs = tiles[0, 0]
    yt, away, own_sum, row_aux, col_aux = tile_sums(where, meta, slabs, row_panels, col_panels)
    got = lax.ppermute(away, "col", CORE)
    coded_y, power_y = code_y(meta, col_aux, yt)
    coded = code_x(meta, row_aux, own_sum, got, coded_y, power_y)
    moved = lax.all_to_all(coded, both, 0, 0, tiled=True)
    return solve_rows(moved, gram_inverse)


def solution(mesh):
    in_specs = (
        P("row", "col", None, None, None),
        P("row", "col", None, None),
        P("row", "col"),
        P(("row", "col"), None),
        P(("row", "col")),
        P(),
    )

    return jax.shard_map(
        per_device,
        mesh=mesh,
        in_specs=in_specs,
        out_specs=P(("row", "col"), None),
        check_vma=False,
    )
```

```python
import jax
import jax.numpy as jnp
from jax import lax
from jax.experimental import pallas as pl
from jax.experimental.pallas import tpu as pltpu
from jax.sharding import PartitionSpec as P


K = 256
T = 256
TR = 16
TC = 8
NNZ = 96
CHUNK = 16
AUX = 16
BLK = T + AUX
DEV = 128
ROWS = 72
HI = lax.Precision.HIGHEST
VMEM = pl.BlockSpec(memory_space=pltpu.VMEM)
SMEM = pl.BlockSpec(memory_space=pltpu.SMEM)
F32 = jnp.float32
BF16 = jnp.bfloat16


def position(meta):
    row_at, col_at = meta[1], meta[2]
    chip = col_at // 2
    return (
        lax.rem(col_at, 2),
        chip // 2,
        lax.rem(chip, 2),
        row_at // 4,
        lax.rem(row_at, 4),
    )


def row_panel_at(meta, n):
    core, x_at, y_at, _, _ = position(meta)
    xx = lax.rem(x_at + 4 - (n // 2) % 4, 4)
    yy = 1 - y_at if n % 2 else y_at
    hh = 1 - core if n // 8 else core
    return xx * 4 + yy * 2 + hh


def col_panel_at(meta, n):
    _, _, _, lo_at, z_at = position(meta)
    zz = lax.rem(z_at + 4 - n // 2, 4)
    return (1 - lo_at if n % 2 else lo_at) * 4 + zz


def block_kernel(factors, owner, out_ref):
    home, slot = owner[...] // T, lax.rem(owner[...], T)
    same = (lax.broadcasted_iota(jnp.int32, (DEV, T), 0) == home).astype(BF16)
    before = (
        lax.broadcasted_iota(jnp.int32, (T, T), 0) < lax.broadcasted_iota(jnp.int32, (T, T), 1)
    ).astype(BF16)
    earlier = jnp.dot(same, before, preferred_element_type=F32) * same.astype(F32)
    place = jnp.sum(earlier, axis=0, keepdims=True) * DEV + home.astype(F32)
    line = lax.broadcasted_iota(jnp.int32, (AUX, T), 0)
    extra = jnp.where(line == 0, place, jnp.where(line == 1, slot.astype(F32), 0.0))
    out_ref[0:T, :] = factors[...]
    out_ref[T:BLK, :] = extra.astype(BF16)


def make_block(factors, owner):
    return pl.pallas_call(
        block_kernel,
        out_shape=jax.ShapeDtypeStruct((BLK, T), BF16),
        in_specs=[VMEM] * 2,
        out_specs=VMEM,
        compiler_params=pltpu.CompilerParams(vmem_limit_bytes=4 << 20),
        name="make_block",
    )(factors, owner.reshape(1, T))


def chunk_copy(tiles, held, sems, c):
    at = pl.ds(c * CHUNK, CHUNK)
    return pltpu.make_async_copy(tiles.at[at], held.at[at], sems.at[c])


def over_tiles(count, tiles, held, sems, fill, step):
    for c in range(NNZ // CHUNK):
        chunk_copy(tiles, held, sems, c).start()
    fill()

    def chunk(c, _):
        chunk_copy(tiles, held, sems, c).wait()
        for u in range(CHUNK):
            step(c * CHUNK + u)
        return 0

    chunks = (count + CHUNK - 1) // CHUNK
    lax.fori_loop(0, chunks, chunk, 0)

    def rest(c, _):
        chunk_copy(tiles, held, sems, c).wait()
        return 0

    lax.fori_loop(chunks, NNZ // CHUNK, rest, 0)


def tile_kernel(where, meta, tiles, *refs):
    row_panels, col_panels, refs = refs[:8], refs[8:16], refs[16:]
    yt_ref, away_ref, own_ref, row_aux, col_aux, rt, cmat, total, held, sems = refs
    count, first, left = meta[0], meta[1] * TR, meta[2] * TC
    shift = TC * (1 - position(meta)[0])

    def fill():
        yt_ref[...] = jnp.zeros_like(yt_ref)
        total[...] = jnp.zeros_like(total)
        rt[TR] = jnp.zeros((K, T), BF16)
        cmat[TC] = jnp.zeros((T, K), BF16)
        for n in range(8):
            at = col_panel_at(meta, n)
            cmat[at] = col_panels[n][0:T, :]
            col_aux[at] = col_panels[n][T:BLK, :]
        for n in range(16):
            at = row_panel_at(meta, n)
            rt[at] = row_panels[n // 2][n % 2, 0:T, :].T
            row_aux[at] = row_panels[n // 2][n % 2, T:BLK, :]

    def step(s):
        i, j = where[2 * s], where[2 * s + 1]
        use = s < count
        upper = jnp.logical_and(use, first + i < left + j)
        at = lax.rem(jnp.where(use, i, 0) + shift, TR)
        total[at] += jnp.dot(
            held[s], cmat[jnp.where(use, j, TC)], preferred_element_type=F32
        )
        at = pl.multiple_of(jnp.where(upper, j, 0) * K, K)
        yt_ref[pl.ds(at, K), :] += jnp.dot(
            rt[jnp.where(upper, i, TR)], held[s], preferred_element_type=F32
        )

    over_tiles(count, tiles, held, sems, fill, step)
    for b in range(TC):
        away_ref[b * T : (b + 1) * T, :] = total[b]
        own_ref[b * T : (b + 1) * T, :] = total[TC + b]


def tile_sums(where, meta, tiles, row_panels, col_panels):
    shapes = [jax.ShapeDtypeStruct((TC * T, K), F32)] * 3
    shapes += [jax.ShapeDtypeStruct((n, AUX, T), BF16) for n in (TR, TC)]
    return pl.pallas_call(
        tile_kernel,
        out_shape=shapes,
        in_specs=[SMEM, SMEM, pl.BlockSpec(memory_space=pltpu.HBM)] + [VMEM] * 16,
        out_specs=[VMEM] * 5,
        scratch_shapes=[
            pltpu.VMEM((TR + 1, K, T), BF16),
            pltpu.VMEM((TC + 1, T, K), BF16),
            pltpu.VMEM((TR, T, K), F32),
            pltpu.VMEM((NNZ, T, T), BF16),
            pltpu.SemaphoreType.DMA((NNZ // CHUNK,)),
        ],
        cost_estimate=pl.CostEstimate(
            flops=6_500_000_000, bytes_accessed=20_000_000, transcendentals=0
        ),
        compiler_params=pltpu.CompilerParams(vmem_limit_bytes=53 << 20),
        name="tile_sums",
    )(where, meta, tiles, *row_panels, *col_panels)


def split_dot(pick, value, dims):
    high = value.astype(BF16)
    low = (value - high.astype(F32)).astype(BF16)
    first = lax.dot_general(pick, high, dims, preferred_element_type=F32)
    return first + lax.dot_general(pick, low, dims, preferred_element_type=F32)


NN, NT = (((1,), (0,)), ((), ())), (((1,), (1,)), ((), ()))


def code(value):
    return jnp.floor(value + 0.5).astype(jnp.int32).astype(jnp.int16)


def sort_panel(is_x, meta, aux, rows, stride, block):
    core = position(meta)[0]
    base = TC * core if is_x else 0
    offset = lax.rem(2 * meta[1] + core, 8) * 16
    places = lax.broadcasted_iota(jnp.int32, (DEV, T), 0).astype(F32)
    lane_ids = lax.broadcasted_iota(jnp.int32, (128, T), 0)
    peak = jnp.zeros((8, 128), F32)
    slots = jnp.zeros((DEV, 128), F32)
    for b in range(TC):
        extra = aux[base + b].astype(F32)
        value = block(b)
        for t in range(2):
            pick = (extra[0:1, :] - float(t * DEV) == places).astype(BF16)
            moved = split_dot(pick, value, NN if is_x else NT)
            for side in range(2):
                half = moved[:, side * 128 : (side + 1) * 128]
                peak = jnp.maximum(peak, jnp.max(jnp.abs(half.reshape(16, 8, 128)), axis=0))
                rows[pl.ds(16 * side + 2 * b + t, DEV, stride=stride), :] = half
            if is_x:
                lanes = jnp.where(lane_ids == offset + (2 * b + t), extra[1:2, :], 0.0)
                slots += lax.dot_general(
                    pick, lanes.astype(BF16), NT, preferred_element_type=F32
                )
    top = jnp.broadcast_to(
        jnp.maximum(jnp.max(peak, axis=(0, 1), keepdims=True), 1e-30), (8, 128)
    )
    power = jnp.clip(jnp.floor(jnp.log2(32000.0 / top)), -100.0, 100.0)
    return power, jnp.exp2(power)[0:1, :], slots


def code_y_kernel(meta, aux, yt, out_ref, power_ref, rows):
    power, scale, _ = sort_panel(
        False, meta, aux, rows, 32, lambda b: yt[b * T : (b + 1) * T, :]
    )
    power_ref[...] = power

    def to_one(d, _):
        out_ref[d] = code(rows[pl.ds(pl.multiple_of(d * 32, 32), 32), :] * scale)
        return 0

    lax.fori_loop(0, DEV, to_one, 0, unroll=8)


def code_y(meta, aux, yt):
    return pl.pallas_call(
        code_y_kernel,
        out_shape=(
            jax.ShapeDtypeStruct((DEV, 32, 128), jnp.int16),
            jax.ShapeDtypeStruct((8, 128), F32),
        ),
        in_specs=[SMEM] + [VMEM] * 2,
        out_specs=(VMEM, VMEM),
        scratch_shapes=[pltpu.VMEM((DEV * 32, 128), F32)],
        cost_estimate=pl.CostEstimate(
            flops=1_000_000_000, bytes_accessed=8_000_000, transcendentals=0
        ),
        compiler_params=pltpu.CompilerParams(vmem_limit_bytes=8 << 20),
        name="code_y",
    )(meta, aux, yt)


def code_x_kernel(meta, aux, own, got, coded_y, power_y, out_ref, rows):
    def block(b):
        at = slice(b * T, (b + 1) * T)
        return own[at, :] + got[at, :]

    power, scale, slots = sort_panel(True, meta, aux, rows, 40, block)
    low_half = 2 * meta[1] + position(meta)[0] < 8
    rows[pl.ds(32, DEV, stride=40), :] = jnp.where(low_half, slots, 0.0)
    rows[pl.ds(33, DEV, stride=40), :] = jnp.where(low_half, 0.0, slots)
    rows[pl.ds(34, DEV, stride=40), :] = jnp.broadcast_to(power[0:1, :], (DEV, 128))
    rows[pl.ds(35, DEV, stride=40), :] = jnp.broadcast_to(power_y[0:1, :], (DEV, 128))
    for line in range(36, 40):
        rows[pl.ds(line, DEV, stride=40), :] = jnp.zeros((DEV, 128), F32)

    def to_one(d, _):
        at = pl.multiple_of(d * 40, 8)
        out_ref[d, 0:32, :] = code(rows[pl.ds(at, 32), :] * scale)
        out_ref[d, 32:64, :] = coded_y[d]
        out_ref[d, 64:ROWS, :] = code(rows[pl.ds(at + 32, 8), :])
        return 0

    lax.fori_loop(0, DEV, to_one, 0, unroll=8)


def code_x(meta, aux, own, got, coded_y, power_y):
    return pl.pallas_call(
        code_x_kernel,
        out_shape=jax.ShapeDtypeStruct((DEV, ROWS, 128), jnp.int16),
        in_specs=[SMEM] + [VMEM] * 5,
        out_specs=VMEM,
        scratch_shapes=[pltpu.VMEM((DEV * 40, 128), F32)],
        cost_estimate=pl.CostEstimate(
            flops=1_000_000_000, bytes_accessed=8_000_000, transcendentals=0
        ),
        compiler_params=pltpu.CompilerParams(vmem_limit_bytes=8 << 20),
        name="code_x",
    )(meta, aux, own, got, coded_y, power_y)


def solve_kernel(got, gram, out_ref, sums, slots):
    sums[...] = jnp.zeros_like(sums)
    slots[...] = jnp.zeros_like(slots)

    def source_row(r, _):
        totals = [sums[2 * r], sums[2 * r + 1]]
        for c in range(16):
            value = got[r * 16 + c].astype(jnp.int32).astype(F32)
            totals[c % 2] += value[0:32, :] * jnp.exp2(-value[66:67, :])
            if c < 2:
                slots[...] += value[64:72, :]
        sums[2 * r] = totals[0]
        sums[2 * r + 1] = totals[1]
        for c in range(16):
            value = got[r * 16 + c].astype(jnp.int32).astype(F32)
            sums[c] += value[32:64, :] * jnp.exp2(-value[67:68, :])
        return 0

    lax.fori_loop(0, 8, source_row, 0)
    product = jnp.concatenate(
        [sums[:, 0:16, :].reshape(256, 128), sums[:, 16:32, :].reshape(256, 128)], axis=1
    )
    where = jnp.concatenate([slots[0:1, :], slots[1:2, :]], axis=1)
    ids = lax.broadcasted_iota(jnp.int32, (256, 256), 0).astype(F32)
    pick = (ids == where).astype(F32)
    placed = jnp.dot(pick, product, precision=HI, preferred_element_type=F32)
    out_ref[...] = jnp.dot(placed, gram[...], precision=HI, preferred_element_type=F32)


def solve_rows(got, gram):
    return pl.pallas_call(
        solve_kernel,
        out_shape=jax.ShapeDtypeStruct((256, 256), F32),
        in_specs=[VMEM] * 2,
        out_specs=VMEM,
        scratch_shapes=[pltpu.VMEM((16, 32, 128), F32), pltpu.VMEM((8, 128), F32)],
        compiler_params=pltpu.CompilerParams(vmem_limit_bytes=8 << 20),
        name="solve_rows",
    )(got, gram)


def along_x(shift):
    return [(c, (c + 4 * shift) % 16) for c in range(16)]


def along_z(shift):
    return [(r, (r // 4) * 4 + (r + shift) % 4) for r in range(8)]


CORE = [(c, c ^ 1) for c in range(16)]
UPPER_Y = [(c, c ^ 2) for c in range(16)]
LOWER_Y = [(r, r ^ 4) for r in range(8)]
TO_COLUMN = [
    (16 * r + c, 16 * (c % 8) + 2 * r + c // 8) for r in range(8) for c in range(16)
]


def per_device(tiles, tile_coord, tile_count, factors, owner, gram_inverse):
    both = ("row", "col")
    block = make_block(factors, owner)

    row_pair = jnp.stack([block, lax.ppermute(block, "col", UPPER_Y)])
    own = [row_pair] + [lax.ppermute(row_pair, "col", along_x(s)) for s in (1, 2, 3)]
    row_panels = own + [lax.ppermute(own[n], "col", CORE) for n in range(4)]
    first = lax.ppermute(block, both, TO_COLUMN)
    lower = lax.ppermute(first, "row", LOWER_Y)
    col_panels = [first, lower]
    for s in (1, 2, 3):
        col_panels += [
            lax.ppermute(first, "row", along_z(s)), lax.ppermute(lower, "row", along_z(s))
        ]

    row_at, col_at = lax.axis_index("row"), lax.axis_index("col")
    meta = jnp.stack([tile_count[0, 0], row_at, col_at]).astype(jnp.int32)
    where = tile_coord[0, 0].reshape(-1)
    slabs = tiles[0, 0]
    yt, away, own_sum, row_aux, col_aux = tile_sums(where, meta, slabs, row_panels, col_panels)
    got = lax.ppermute(away, "col", CORE)
    coded_y, power_y = code_y(meta, col_aux, yt)
    coded = code_x(meta, row_aux, own_sum, got, coded_y, power_y)
    moved = lax.all_to_all(coded, both, 0, 0, tiled=True)
    return solve_rows(moved, gram_inverse)


def solution(mesh):
    in_specs = (
        P("row", "col", None, None, None),
        P("row", "col", None, None),
        P("row", "col"),
        P(("row", "col"), None),
        P(("row", "col")),
        P(),
    )

    return jax.shard_map(
        per_device,
        mesh=mesh,
        in_specs=in_specs,
        out_specs=P(("row", "col"), None),
        check_vma=False,
    )
```

```python
import jax
import jax.numpy as jnp
from jax import lax
from jax.experimental import pallas as pl
from jax.experimental.pallas import tpu as pltpu
from jax.sharding import PartitionSpec as P


K = 256
T = 256
TR = 16
TC = 8
NNZ = 96
CHUNK = 16
AUX = 8
BLK = T + AUX
DEV = 128
ROWS = 72
HI = lax.Precision.HIGHEST
VMEM = pl.BlockSpec(memory_space=pltpu.VMEM)
SMEM = pl.BlockSpec(memory_space=pltpu.SMEM)
F32 = jnp.float32
BF16 = jnp.bfloat16


def position(meta):
    row_at, col_at = meta[1], meta[2]
    chip = col_at // 2
    return (
        lax.rem(col_at, 2),
        chip // 2,
        lax.rem(chip, 2),
        row_at // 4,
        lax.rem(row_at, 4),
    )


def row_panel_at(meta, n):
    core, x_at, y_at, _, _ = position(meta)
    xx = lax.rem(x_at + 4 - (n // 2) % 4, 4)
    yy = 1 - y_at if n % 2 else y_at
    hh = 1 - core if n // 8 else core
    return xx * 4 + yy * 2 + hh


def col_panel_at(meta, n):
    _, _, _, lo_at, z_at = position(meta)
    zz = lax.rem(z_at + 4 - n // 2, 4)
    return (1 - lo_at if n % 2 else lo_at) * 4 + zz


def block_kernel(factors, owner, out_ref):
    home, slot = owner[...] // T, lax.rem(owner[...], T)
    same = (lax.broadcasted_iota(jnp.int32, (DEV, T), 0) == home).astype(BF16)
    before = (
        lax.broadcasted_iota(jnp.int32, (T, T), 0) < lax.broadcasted_iota(jnp.int32, (T, T), 1)
    ).astype(BF16)
    earlier = jnp.dot(same, before, preferred_element_type=F32) * same.astype(F32)
    place = jnp.sum(earlier, axis=0, keepdims=True) * DEV + home.astype(F32)
    line = lax.broadcasted_iota(jnp.int32, (AUX, T), 0)
    extra = jnp.where(line == 0, place, jnp.where(line == 1, slot.astype(F32), 0.0))
    out_ref[0:T, :] = factors[...]
    out_ref[T:BLK, :] = extra.astype(BF16)


def make_block(factors, owner):
    return pl.pallas_call(
        block_kernel,
        out_shape=jax.ShapeDtypeStruct((BLK, T), BF16),
        in_specs=[VMEM] * 2,
        out_specs=VMEM,
        compiler_params=pltpu.CompilerParams(vmem_limit_bytes=4 << 20),
        name="make_block",
    )(factors, owner.reshape(1, T))


def code(value):
    return jnp.floor(value + 0.5).astype(jnp.int32).astype(jnp.int16)


def scale_of(peak):
    top = jnp.broadcast_to(
        jnp.maximum(jnp.max(peak, axis=(0, 1), keepdims=True), 1e-30), (8, 128)
    )
    power = jnp.clip(jnp.floor(jnp.log2(32000.0 / top)), -100.0, 100.0)
    return power, jnp.exp2(power)[0:1, :]


def chunk_copy(tiles, held, sems, c):
    at = pl.ds(c * CHUNK, CHUNK)
    return pltpu.make_async_copy(tiles.at[at], held.at[at], sems.at[c])


def over_tiles(count, tiles, held, sems, fill, step):
    for c in range(NNZ // CHUNK):
        chunk_copy(tiles, held, sems, c).start()
    fill()

    def chunk(c, _):
        chunk_copy(tiles, held, sems, c).wait()
        for u in range(CHUNK):
            step(c * CHUNK + u)
        return 0

    chunks = (count + CHUNK - 1) // CHUNK
    lax.fori_loop(0, chunks, chunk, 0)

    def rest(c, _):
        chunk_copy(tiles, held, sems, c).wait()
        return 0

    lax.fori_loop(chunks, NNZ // CHUNK, rest, 0)


def tile_kernel(where, meta, tiles, *refs):
    row_panels, col_panels, refs = refs[:8], refs[8:16], refs[16:]
    yq_ref, power_ref, away_ref, own_ref, row_aux, col_aux = refs[:6]
    rt, cmat, total, yt, held, sems = refs[6:]
    count, first, left = meta[0], meta[1] * TR, meta[2] * TC
    shift = TC * (1 - position(meta)[0])

    def fill():
        yt[...] = jnp.zeros_like(yt)
        total[...] = jnp.zeros_like(total)
        rt[TR] = jnp.zeros((K, T), BF16)
        cmat[TC] = jnp.zeros((T, K), BF16)
        for n in range(8):
            at = col_panel_at(meta, n)
            cmat[at] = col_panels[n][0:T, :]
            col_aux[at] = col_panels[n][T:BLK, :]
        for n in range(16):
            at = row_panel_at(meta, n)
            rt[at] = row_panels[n // 2][n % 2, 0:T, :].T
            row_aux[at] = row_panels[n // 2][n % 2, T:BLK, :]

    def step(s):
        i, j = where[2 * s], where[2 * s + 1]
        use = s < count
        upper = jnp.logical_and(use, first + i < left + j)
        at = lax.rem(jnp.where(use, i, 0) + shift, TR)
        total[at] += jnp.dot(
            held[s], cmat[jnp.where(use, j, TC)], preferred_element_type=F32
        )
        yt[jnp.where(upper, j, 0)] += jnp.dot(
            rt[jnp.where(upper, i, TR)], held[s], preferred_element_type=F32
        )

    over_tiles(count, tiles, held, sems, fill, step)
    for b in range(TC):
        away_ref[b * T : (b + 1) * T, :] = total[b]
        own_ref[b * T : (b + 1) * T, :] = total[TC + b]
    peak = jnp.zeros((8, 128), F32)
    for b in range(TC):
        for side in range(2):
            half = jnp.abs(yt[b, :, side * 128 : (side + 1) * 128])
            peak = jnp.maximum(peak, jnp.max(half.reshape(K // 8, 8, 128), axis=0))
    power, scale = scale_of(peak)
    power_ref[...] = power
    scale = jnp.concatenate([scale, scale], axis=1)
    for b in range(TC):
        yq_ref[b] = code(yt[b] * scale)


def tile_sums(where, meta, tiles, row_panels, col_panels):
    shapes = [
        jax.ShapeDtypeStruct((TC, K, T), jnp.int16),
        jax.ShapeDtypeStruct((8, 128), F32),
    ]
    shapes += [jax.ShapeDtypeStruct((TC * T, K), F32)] * 2
    shapes += [jax.ShapeDtypeStruct((n, AUX, T), BF16) for n in (TR, TC)]
    return pl.pallas_call(
        tile_kernel,
        out_shape=shapes,
        in_specs=[SMEM, SMEM, pl.BlockSpec(memory_space=pltpu.HBM)] + [VMEM] * 16,
        out_specs=[VMEM] * 6,
        scratch_shapes=[
            pltpu.VMEM((TR + 1, K, T), BF16),
            pltpu.VMEM((TC + 1, T, K), BF16),
            pltpu.VMEM((TR, T, K), F32),
            pltpu.VMEM((TC, K, T), F32),
            pltpu.VMEM((NNZ, T, T), BF16),
            pltpu.SemaphoreType.DMA((NNZ // CHUNK,)),
        ],
        cost_estimate=pl.CostEstimate(
            flops=6_500_000_000, bytes_accessed=20_000_000, transcendentals=0
        ),
        compiler_params=pltpu.CompilerParams(vmem_limit_bytes=53 << 20),
        name="tile_sums",
    )(where, meta, tiles, *row_panels, *col_panels)


def split_dot(pick, value, dims):
    high = value.astype(BF16)
    low = (value - high.astype(F32)).astype(BF16)
    first = lax.dot_general(pick, high, dims, preferred_element_type=F32)
    return first + lax.dot_general(pick, low, dims, preferred_element_type=F32)


NN, NT = (((1,), (0,)), ((), ())), (((1,), (1,)), ((), ()))


def integer_dot(pick, value):
    whole = value.astype(jnp.int32)
    high, low = (whole >> 8).astype(F32).astype(BF16), (whole & 255).astype(F32).astype(BF16)
    first = lax.dot_general(pick, high, NT, preferred_element_type=F32)
    return first * 256.0 + lax.dot_general(pick, low, NT, preferred_element_type=F32)


def sort_panel(is_x, meta, aux, rows, stride, block):
    core = position(meta)[0]
    base = TC * core if is_x else 0
    offset = lax.rem(2 * meta[1] + core, 8) * 16
    places = lax.broadcasted_iota(jnp.int32, (DEV, T), 0).astype(F32)
    lane_ids = lax.broadcasted_iota(jnp.int32, (128, T), 0)
    peak = jnp.zeros((8, 128), F32)
    slots = jnp.zeros((DEV, 128), F32)
    for b in range(TC):
        extra = aux[base + b].astype(F32)
        value = block(b)
        for t in range(2):
            pick = (extra[0:1, :] - float(t * DEV) == places).astype(BF16)
            moved = (split_dot(pick, value, NN) if is_x else integer_dot(pick, value))
            for side in range(2):
                half = moved[:, side * 128 : (side + 1) * 128]
                if is_x:
                    top = jnp.max(jnp.abs(half.reshape(16, 8, 128)), axis=0)
                    peak = jnp.maximum(peak, top)
                rows[pl.ds(16 * side + 2 * b + t, DEV, stride=stride), :] = half
            if is_x:
                lanes = jnp.where(lane_ids == offset + (2 * b + t), extra[1:2, :], 0.0)
                slots += lax.dot_general(
                    pick, lanes.astype(BF16), NT, preferred_element_type=F32
                )
    return peak, slots


def code_y_kernel(meta, aux, yq, out_ref, rows):
    sort_panel(False, meta, aux, rows, 32, lambda b: yq[b])

    def to_one(d, _):
        value = rows[pl.ds(pl.multiple_of(d * 32, 32), 32), :]
        out_ref[d] = value.astype(jnp.int32).astype(jnp.int16)
        return 0

    lax.fori_loop(0, DEV, to_one, 0, unroll=8)


def code_y(meta, aux, yq):
    return pl.pallas_call(
        code_y_kernel,
        out_shape=jax.ShapeDtypeStruct((DEV, 32, 128), jnp.int16),
        in_specs=[SMEM] + [VMEM] * 2,
        out_specs=VMEM,
        scratch_shapes=[pltpu.VMEM((DEV * 32, 128), F32)],
        cost_estimate=pl.CostEstimate(
            flops=1_000_000_000, bytes_accessed=8_000_000, transcendentals=0
        ),
        compiler_params=pltpu.CompilerParams(vmem_limit_bytes=8 << 20),
        name="code_y",
    )(meta, aux, yq)


def code_x_kernel(meta, aux, own, got, coded_y, power_y, out_ref, rows):
    def block(b):
        at = slice(b * T, (b + 1) * T)
        return own[at, :] + got[at, :]

    peak, slots = sort_panel(True, meta, aux, rows, 40, block)
    power, scale = scale_of(peak)
    low_half = 2 * meta[1] + position(meta)[0] < 8
    rows[pl.ds(32, DEV, stride=40), :] = jnp.where(low_half, slots, 0.0)
    rows[pl.ds(33, DEV, stride=40), :] = jnp.where(low_half, 0.0, slots)
    rows[pl.ds(34, DEV, stride=40), :] = jnp.broadcast_to(power[0:1, :], (DEV, 128))
    rows[pl.ds(35, DEV, stride=40), :] = jnp.broadcast_to(power_y[0:1, :], (DEV, 128))
    for line in range(36, 40):
        rows[pl.ds(line, DEV, stride=40), :] = jnp.zeros((DEV, 128), F32)

    def to_one(d, _):
        at = pl.multiple_of(d * 40, 8)
        out_ref[d, 0:32, :] = code(rows[pl.ds(at, 32), :] * scale)
        out_ref[d, 32:64, :] = coded_y[d]
        out_ref[d, 64:ROWS, :] = code(rows[pl.ds(at + 32, 8), :])
        return 0

    lax.fori_loop(0, DEV, to_one, 0, unroll=8)


def code_x(meta, aux, own, got, coded_y, power_y):
    return pl.pallas_call(
        code_x_kernel,
        out_shape=jax.ShapeDtypeStruct((DEV, ROWS, 128), jnp.int16),
        in_specs=[SMEM] + [VMEM] * 5,
        out_specs=VMEM,
        scratch_shapes=[pltpu.VMEM((DEV * 40, 128), F32)],
        cost_estimate=pl.CostEstimate(
            flops=1_000_000_000, bytes_accessed=8_000_000, transcendentals=0
        ),
        compiler_params=pltpu.CompilerParams(vmem_limit_bytes=8 << 20),
        name="code_x",
    )(meta, aux, own, got, coded_y, power_y)


def solve_kernel(got, gram, out_ref, sums, slots):
    sums[...] = jnp.zeros_like(sums)
    slots[...] = jnp.zeros_like(slots)

    def source_row(r, _):
        totals = [sums[2 * r], sums[2 * r + 1]]
        for c in range(16):
            value = got[r * 16 + c].astype(jnp.int32).astype(F32)
            totals[c % 2] += value[0:32, :] * jnp.exp2(-value[66:67, :])
            if c < 2:
                slots[...] += value[64:72, :]
        sums[2 * r] = totals[0]
        sums[2 * r + 1] = totals[1]
        for c in range(16):
            value = got[r * 16 + c].astype(jnp.int32).astype(F32)
            sums[c] += value[32:64, :] * jnp.exp2(-value[67:68, :])
        return 0

    lax.fori_loop(0, 8, source_row, 0)
    product = jnp.concatenate(
        [sums[:, 0:16, :].reshape(256, 128), sums[:, 16:32, :].reshape(256, 128)], axis=1
    )
    where = jnp.concatenate([slots[0:1, :], slots[1:2, :]], axis=1)
    ids = lax.broadcasted_iota(jnp.int32, (256, 256), 0).astype(F32)
    pick = (ids == where).astype(F32)
    placed = jnp.dot(pick, product, precision=HI, preferred_element_type=F32)
    out_ref[...] = jnp.dot(placed, gram[...], precision=HI, preferred_element_type=F32)


def solve_rows(got, gram):
    return pl.pallas_call(
        solve_kernel,
        out_shape=jax.ShapeDtypeStruct((256, 256), F32),
        in_specs=[VMEM] * 2,
        out_specs=VMEM,
        scratch_shapes=[pltpu.VMEM((16, 32, 128), F32), pltpu.VMEM((8, 128), F32)],
        compiler_params=pltpu.CompilerParams(vmem_limit_bytes=8 << 20),
        name="solve_rows",
    )(got, gram)


def along_x(shift):
    return [(c, (c + 4 * shift) % 16) for c in range(16)]


def along_z(shift):
    return [(r, (r // 4) * 4 + (r + shift) % 4) for r in range(8)]


CORE = [(c, c ^ 1) for c in range(16)]
UPPER_Y = [(c, c ^ 2) for c in range(16)]
LOWER_Y = [(r, r ^ 4) for r in range(8)]
TO_COLUMN = [
    (16 * r + c, 16 * (c % 8) + 2 * r + c // 8) for r in range(8) for c in range(16)
]


def per_device(tiles, tile_coord, tile_count, factors, owner, gram_inverse):
    both = ("row", "col")
    block = make_block(factors, owner)

    row_pair = jnp.stack([block, lax.ppermute(block, "col", UPPER_Y)])
    flat = tile_coord[0, 0].reshape(-1)
    row_pair, where = lax.optimization_barrier((row_pair, flat))
    own = [row_pair] + [lax.ppermute(row_pair, "col", along_x(s)) for s in (1, 2, 3)]
    row_panels = own + [lax.ppermute(own[n], "col", CORE) for n in range(4)]
    first = lax.ppermute(block, both, TO_COLUMN)
    lower = lax.ppermute(first, "row", LOWER_Y)
    col_panels = [first, lower]
    for s in (1, 2, 3):
        col_panels += [
            lax.ppermute(first, "row", along_z(s)), lax.ppermute(lower, "row", along_z(s))
        ]

    row_at, col_at = lax.axis_index("row"), lax.axis_index("col")
    meta = jnp.stack([tile_count[0, 0], row_at, col_at]).astype(jnp.int32)
    slabs = tiles[0, 0]
    yq, power_y, away, own_sum, row_aux, col_aux = tile_sums(where, meta, slabs, row_panels, col_panels)
    got = lax.ppermute(away, "col", CORE)
    coded_y = code_y(meta, col_aux, yq)
    coded = code_x(meta, row_aux, own_sum, got, coded_y, power_y)
    moved = lax.all_to_all(coded, both, 0, 0, tiled=True)
    return solve_rows(moved, gram_inverse)


def solution(mesh):
    in_specs = (
        P("row", "col", None, None, None),
        P("row", "col", None, None),
        P("row", "col"),
        P(("row", "col"), None),
        P(("row", "col")),
        P(),
    )

    return jax.shard_map(
        per_device,
        mesh=mesh,
        in_specs=in_specs,
        out_specs=P(("row", "col"), None),
        check_vma=False,
    )
```

```python
import jax
import jax.numpy as jnp
from jax import lax
from jax.experimental import pallas as pl
from jax.experimental.pallas import tpu as pltpu
from jax.sharding import PartitionSpec as P


K = 256
T = 256
TR = 16
TC = 8
NNZ = 96
CHUNK = 16
AUX = 8
BLK = T + AUX
DEV = 128
ROWS = 72
HI = lax.Precision.HIGHEST
VMEM = pl.BlockSpec(memory_space=pltpu.VMEM)
SMEM = pl.BlockSpec(memory_space=pltpu.SMEM)
F32 = jnp.float32
BF16 = jnp.bfloat16


def position(meta):
    row_at, col_at = meta[1], meta[2]
    chip = col_at // 2
    return (
        lax.rem(col_at, 2),
        chip // 2,
        lax.rem(chip, 2),
        row_at // 4,
        lax.rem(row_at, 4),
    )


def row_panel_at(meta, n):
    core, x_at, y_at, _, _ = position(meta)
    xx = lax.rem(x_at + 4 - (n // 2) % 4, 4)
    yy = 1 - y_at if n % 2 else y_at
    hh = 1 - core if n // 8 else core
    return xx * 4 + yy * 2 + hh


def col_panel_at(meta, n):
    _, _, _, lo_at, z_at = position(meta)
    zz = lax.rem(z_at + 4 - n // 2, 4)
    return (1 - lo_at if n % 2 else lo_at) * 4 + zz


def block_kernel(factors, owner, out_ref):
    home, slot = owner[...] // T, lax.rem(owner[...], T)
    same = (lax.broadcasted_iota(jnp.int32, (DEV, T), 0) == home).astype(BF16)
    before = (
        lax.broadcasted_iota(jnp.int32, (T, T), 0) < lax.broadcasted_iota(jnp.int32, (T, T), 1)
    ).astype(BF16)
    earlier = jnp.dot(same, before, preferred_element_type=F32) * same.astype(F32)
    place = jnp.sum(earlier, axis=0, keepdims=True) * DEV + home.astype(F32)
    line = lax.broadcasted_iota(jnp.int32, (AUX, T), 0)
    extra = jnp.where(line == 0, place, jnp.where(line == 1, slot.astype(F32), 0.0))
    out_ref[0:T, :] = factors[...]
    out_ref[T:BLK, :] = extra.astype(BF16)


def make_block(factors, owner):
    return pl.pallas_call(
        block_kernel,
        out_shape=jax.ShapeDtypeStruct((BLK, T), BF16),
        in_specs=[VMEM] * 2,
        out_specs=VMEM,
        compiler_params=pltpu.CompilerParams(vmem_limit_bytes=4 << 20),
        name="make_block",
    )(factors, owner.reshape(1, T))


def code(value):
    return jnp.floor(value + 0.5).astype(jnp.int32).astype(jnp.int16)


def scale_of(peak):
    top = jnp.broadcast_to(
        jnp.maximum(jnp.max(peak, axis=(0, 1), keepdims=True), 1e-30), (8, 128)
    )
    power = jnp.clip(jnp.floor(jnp.log2(32000.0 / top)), -100.0, 100.0)
    return power, jnp.exp2(power)[0:1, :]


def chunk_copy(tiles, held, sems, c):
    at = pl.ds(c * CHUNK, CHUNK)
    return pltpu.make_async_copy(tiles.at[at], held.at[at], sems.at[c])


def over_tiles(count, tiles, held, sems, fill, step):
    for c in range(NNZ // CHUNK):
        chunk_copy(tiles, held, sems, c).start()
    fill()

    def chunk(c, _):
        chunk_copy(tiles, held, sems, c).wait()
        for u in range(CHUNK):
            step(c * CHUNK + u)
        return 0

    chunks = (count + CHUNK - 1) // CHUNK
    lax.fori_loop(0, chunks, chunk, 0)

    def rest(c, _):
        chunk_copy(tiles, held, sems, c).wait()
        return 0

    lax.fori_loop(chunks, NNZ // CHUNK, rest, 0)


def tile_kernel(where, meta, tiles, *refs):
    row_panels, col_panels, refs = refs[:8], refs[8:16], refs[16:]
    yq_ref, power_ref, away_ref, own_ref, row_aux, col_aux = refs[:6]
    rt, cmat, total, yt, held, sems = refs[6:]
    count, first, left = meta[0], meta[1] * TR, meta[2] * TC
    shift = TC * (1 - position(meta)[0])

    def fill():
        yt[...] = jnp.zeros_like(yt)
        total[...] = jnp.zeros_like(total)
        rt[TR] = jnp.zeros((K, T), BF16)
        cmat[TC] = jnp.zeros((T, K), BF16)
        for n in range(8):
            at = col_panel_at(meta, n)
            cmat[at] = col_panels[n][0:T, :]
            col_aux[at] = col_panels[n][T:BLK, :]
        for n in range(16):
            at = row_panel_at(meta, n)
            rt[at] = row_panels[n // 2][n % 2, 0:T, :].T
            row_aux[at] = row_panels[n // 2][n % 2, T:BLK, :]

    def step(s):
        i, j = where[2 * s], where[2 * s + 1]
        use = s < count
        upper = jnp.logical_and(use, first + i < left + j)
        at = lax.rem(jnp.where(use, i, 0) + shift, TR)
        total[at] += jnp.dot(
            held[s], cmat[jnp.where(use, j, TC)], preferred_element_type=F32
        )
        yt[jnp.where(upper, j, 0)] += jnp.dot(
            rt[jnp.where(upper, i, TR)], held[s], preferred_element_type=F32
        )

    over_tiles(count, tiles, held, sems, fill, step)
    for b in range(TC):
        away_ref[b * T : (b + 1) * T, :] = total[b]
        own_ref[b * T : (b + 1) * T, :] = total[TC + b]
    peak = jnp.zeros((8, 128), F32)
    for b in range(TC):
        for side in range(2):
            half = jnp.abs(yt[b, :, side * 128 : (side + 1) * 128])
            peak = jnp.maximum(peak, jnp.max(half.reshape(K // 8, 8, 128), axis=0))
    power, scale = scale_of(peak)
    power_ref[...] = power
    scale = jnp.concatenate([scale, scale], axis=1)
    for b in range(TC):
        yq_ref[b] = code(yt[b] * scale)


def tile_sums(where, meta, tiles, row_panels, col_panels):
    shapes = [
        jax.ShapeDtypeStruct((TC, K, T), jnp.int16),
        jax.ShapeDtypeStruct((8, 128), F32),
    ]
    shapes += [jax.ShapeDtypeStruct((TC * T, K), F32)] * 2
    shapes += [jax.ShapeDtypeStruct((n, AUX, T), BF16) for n in (TR, TC)]
    return pl.pallas_call(
        tile_kernel,
        out_shape=shapes,
        in_specs=[SMEM, SMEM, pl.BlockSpec(memory_space=pltpu.HBM)] + [VMEM] * 16,
        out_specs=[VMEM] * 6,
        scratch_shapes=[
            pltpu.VMEM((TR + 1, K, T), BF16),
            pltpu.VMEM((TC + 1, T, K), BF16),
            pltpu.VMEM((TR, T, K), F32),
            pltpu.VMEM((TC, K, T), F32),
            pltpu.VMEM((NNZ, T, T), BF16),
            pltpu.SemaphoreType.DMA((NNZ // CHUNK,)),
        ],
        cost_estimate=pl.CostEstimate(
            flops=6_500_000_000, bytes_accessed=20_000_000, transcendentals=0
        ),
        compiler_params=pltpu.CompilerParams(vmem_limit_bytes=53 << 20),
        name="tile_sums",
    )(where, meta, tiles, *row_panels, *col_panels)


def split_dot(pick, value, dims):
    high = value.astype(BF16)
    low = (value - high.astype(F32)).astype(BF16)
    first = lax.dot_general(pick, high, dims, preferred_element_type=F32)
    return first + lax.dot_general(pick, low, dims, preferred_element_type=F32)


NN, NT = (((1,), (0,)), ((), ())), (((1,), (1,)), ((), ()))


def integer_dot(pick, value):
    whole = value.astype(jnp.int32)
    high, low = (whole >> 8).astype(F32).astype(BF16), (whole & 255).astype(F32).astype(BF16)
    first = lax.dot_general(pick, high, NT, preferred_element_type=F32)
    return first * 256.0 + lax.dot_general(pick, low, NT, preferred_element_type=F32)


def sort_panel(is_x, meta, aux, rows, stride, block):
    core = position(meta)[0]
    base = TC * core if is_x else 0
    offset = lax.rem(2 * meta[1] + core, 8) * 16
    places = lax.broadcasted_iota(jnp.int32, (DEV, T), 0).astype(F32)
    lane_ids = lax.broadcasted_iota(jnp.int32, (128, T), 0)
    peak = jnp.zeros((8, 128), F32)
    slots = jnp.zeros((DEV, 128), F32)
    for b in range(TC):
        extra = aux[base + b].astype(F32)
        value = block(b)
        for t in range(2):
            pick = (extra[0:1, :] - float(t * DEV) == places).astype(BF16)
            moved = (split_dot(pick, value, NN) if is_x else integer_dot(pick, value))
            for side in range(2):
                half = moved[:, side * 128 : (side + 1) * 128]
                if is_x:
                    top = jnp.max(jnp.abs(half.reshape(16, 8, 128)), axis=0)
                    peak = jnp.maximum(peak, top)
                rows[pl.ds(16 * side + 2 * b + t, DEV, stride=stride), :] = half
            if is_x:
                lanes = jnp.where(lane_ids == offset + (2 * b + t), extra[1:2, :], 0.0)
                slots += lax.dot_general(
                    pick, lanes.astype(BF16), NT, preferred_element_type=F32
                )
    return peak, slots


def code_y_kernel(meta, aux, yq, out_ref, rows):
    sort_panel(False, meta, aux, rows, 32, lambda b: yq[b])

    def to_one(d, _):
        value = rows[pl.ds(pl.multiple_of(d * 32, 32), 32), :]
        out_ref[d] = value.astype(jnp.int32).astype(jnp.int16)
        return 0

    lax.fori_loop(0, DEV, to_one, 0, unroll=8)


def code_y(meta, aux, yq):
    return pl.pallas_call(
        code_y_kernel,
        out_shape=jax.ShapeDtypeStruct((DEV, 32, 128), jnp.int16),
        in_specs=[SMEM] + [VMEM] * 2,
        out_specs=VMEM,
        scratch_shapes=[pltpu.VMEM((DEV * 32, 128), F32)],
        cost_estimate=pl.CostEstimate(
            flops=1_000_000_000, bytes_accessed=8_000_000, transcendentals=0
        ),
        compiler_params=pltpu.CompilerParams(vmem_limit_bytes=8 << 20),
        name="code_y",
    )(meta, aux, yq)


def code_x_kernel(meta, aux, own, got, coded_y, power_y, out_ref, rows):
    def block(b):
        at = slice(b * T, (b + 1) * T)
        return own[at, :] + got[at, :]

    peak, slots = sort_panel(True, meta, aux, rows, 40, block)
    power, scale = scale_of(peak)
    low_half = 2 * meta[1] + position(meta)[0] < 8
    rows[pl.ds(32, DEV, stride=40), :] = jnp.where(low_half, slots, 0.0)
    rows[pl.ds(33, DEV, stride=40), :] = jnp.where(low_half, 0.0, slots)
    rows[pl.ds(34, DEV, stride=40), :] = jnp.broadcast_to(power[0:1, :], (DEV, 128))
    rows[pl.ds(35, DEV, stride=40), :] = jnp.broadcast_to(power_y[0:1, :], (DEV, 128))
    for line in range(36, 40):
        rows[pl.ds(line, DEV, stride=40), :] = jnp.zeros((DEV, 128), F32)

    def to_one(d, _):
        at = pl.multiple_of(d * 40, 8)
        out_ref[d, 0:32, :] = code(rows[pl.ds(at, 32), :] * scale)
        out_ref[d, 32:64, :] = coded_y[d]
        out_ref[d, 64:ROWS, :] = code(rows[pl.ds(at + 32, 8), :])
        return 0

    lax.fori_loop(0, DEV, to_one, 0, unroll=8)


def code_x(meta, aux, own, got, coded_y, power_y):
    return pl.pallas_call(
        code_x_kernel,
        out_shape=jax.ShapeDtypeStruct((DEV, ROWS, 128), jnp.int16),
        in_specs=[SMEM] + [VMEM] * 5,
        out_specs=VMEM,
        scratch_shapes=[pltpu.VMEM((DEV * 40, 128), F32)],
        cost_estimate=pl.CostEstimate(
            flops=1_000_000_000, bytes_accessed=8_000_000, transcendentals=0
        ),
        compiler_params=pltpu.CompilerParams(vmem_limit_bytes=8 << 20),
        name="code_x",
    )(meta, aux, own, got, coded_y, power_y)


def solve_kernel(got, gram, out_ref, sums, slots):
    slots[...] = jnp.zeros_like(slots)
    for m in range(8):
        for h in range(2):
            total = jnp.zeros((32, 128), F32)
            for chip in range(m, 8):
                value = got[16 * m + 2 * chip + h].astype(jnp.int32).astype(F32)
                total += value[0:32, :] * jnp.exp2(-value[66:67, :])
                if chip == m:
                    slots[...] += value[64:72, :]
            for r in range(m + 1):
                value = got[16 * r + 2 * m + h].astype(jnp.int32).astype(F32)
                total += value[32:64, :] * jnp.exp2(-value[67:68, :])
            sums[2 * m + h] = total
    product = jnp.concatenate(
        [sums[:, 0:16, :].reshape(256, 128), sums[:, 16:32, :].reshape(256, 128)], axis=1
    )
    where = jnp.concatenate([slots[0:1, :], slots[1:2, :]], axis=1)
    ids = lax.broadcasted_iota(jnp.int32, (256, 256), 0).astype(F32)
    pick = (ids == where).astype(F32)
    placed = jnp.dot(pick, product, precision=HI, preferred_element_type=F32)
    out_ref[...] = jnp.dot(placed, gram[...], precision=HI, preferred_element_type=F32)


def solve_rows(got, gram):
    return pl.pallas_call(
        solve_kernel,
        out_shape=jax.ShapeDtypeStruct((256, 256), F32),
        in_specs=[VMEM] * 2,
        out_specs=VMEM,
        scratch_shapes=[pltpu.VMEM((16, 32, 128), F32), pltpu.VMEM((8, 128), F32)],
        compiler_params=pltpu.CompilerParams(vmem_limit_bytes=8 << 20),
        name="solve_rows",
    )(got, gram)


def along_x(shift):
    return [(c, (c + 4 * shift) % 16) for c in range(16)]


def along_z(shift):
    return [(r, (r // 4) * 4 + (r + shift) % 4) for r in range(8)]


CORE = [(c, c ^ 1) for c in range(16)]
UPPER_Y = [(c, c ^ 2) for c in range(16)]
LOWER_Y = [(r, r ^ 4) for r in range(8)]
TO_COLUMN = [
    (16 * r + c, 16 * (c % 8) + 2 * r + c // 8) for r in range(8) for c in range(16)
]


def per_device(tiles, tile_coord, tile_count, factors, owner, gram_inverse):
    both = ("row", "col")
    block = make_block(factors, owner)

    row_pair = jnp.stack([block, lax.ppermute(block, "col", UPPER_Y)])
    flat = tile_coord[0, 0].reshape(-1)
    row_pair, where = lax.optimization_barrier((row_pair, flat))
    own = [row_pair] + [lax.ppermute(row_pair, "col", along_x(s)) for s in (1, 2, 3)]
    row_panels = own + [lax.ppermute(own[n], "col", CORE) for n in range(4)]
    first = lax.ppermute(block, both, TO_COLUMN)
    lower = lax.ppermute(first, "row", LOWER_Y)
    col_panels = [first, lower]
    for s in (1, 2, 3):
        col_panels += [
            lax.ppermute(first, "row", along_z(s)), lax.ppermute(lower, "row", along_z(s))
        ]

    row_at, col_at = lax.axis_index("row"), lax.axis_index("col")
    meta = jnp.stack([tile_count[0, 0], row_at, col_at]).astype(jnp.int32)
    slabs = tiles[0, 0]
    yq, power_y, away, own_sum, row_aux, col_aux = tile_sums(where, meta, slabs, row_panels, col_panels)
    got = lax.ppermute(away, "col", CORE)
    coded_y = code_y(meta, col_aux, yq)
    coded = code_x(meta, row_aux, own_sum, got, coded_y, power_y)
    moved = lax.all_to_all(coded, both, 0, 0, tiled=True)
    return solve_rows(moved, gram_inverse)


def solution(mesh):
    in_specs = (
        P("row", "col", None, None, None),
        P("row", "col", None, None),
        P("row", "col"),
        P(("row", "col"), None),
        P(("row", "col")),
        P(),
    )

    return jax.shard_map(
        per_device,
        mesh=mesh,
        in_specs=in_specs,
        out_specs=P(("row", "col"), None),
        check_vma=False,
    )
```
